512 devices in a mesh: energy: 256 (over z, y, x), slab: 2 (over core).
Axes of the slice: x: 4, y: 8, z: 8, core: 2. Of those that a mesh axis runs over, the one named last changes fastest.
Arguments:
- hamiltonian: float32 [4, 128, 128], P('slab'), may hold values from -2 to 2, as said below
- coupling: float32 [4, 128, 128], P('slab'), may hold values from -0.5 to 0.5
- bonds: int32 [4, 128], P('slab'), may hold values 0 or 1
- phonon_coupling: float32 [4, 128], P('slab'), may hold values from 0.1 to 1
- previous_green: float32 [512, 4, 2, 128], P('energy', 'slab'), may hold values from -2.5 to 2.5, as said below
- phonon_shift: int32 [4], P('slab'), may hold values from 1 to 2
Outputs:
- green_blocks: float32 [512, 4, 2, 128, 128], P('energy', 'slab')
- density: float32 [4, 128], P('slab')
The draws below stay inside these ranges and needn't reach their ends.
Inputs may be any that keep to these rules, and one draw needn't show every extreme that they name: Every hamiltonian block is symmetric. `previous_green`: the imaginary parts (index 1 of the third dimension) are negative.
All inputs are finite; a program needn't handle non-finite values. No bound on the sum of `bonds` on one device may be relied on, other than what follows from the above.
Results may differ from the reference program's by a relative error of at most 0.0001.
Values sent between devices are 32-bit elements; how exact they have to be, the bound alone decides.
A program may use at most 128 MiB of HBM per device.

```python
import math
import jax
import jax.numpy as jnp
from jax import lax

NO = 128
ENER_DEV = 2
ENERGIES = 512
SLABS = 4


def draw_hamiltonian(key, part):
    raw_entries = jax.random.normal(key, (SLABS, NO, NO), jnp.float32)
    symmetric = (raw_entries + jnp.swapaxes(raw_entries, 1, 2)) / jnp.sqrt(2.0 * NO)
    return jnp.clip(symmetric, -2.0, 2.0)


def draw_previous_green(key, part):
    first_key = jax.random.fold_in(key, 11)
    second_key = jax.random.fold_in(key, 23)
    real_part = 0.5 * jax.random.normal(first_key, (ENERGIES, SLABS, NO), jnp.float32)
    imag_part = -jax.random.uniform(second_key, (ENERGIES, SLABS, NO), jnp.float32, 0.05, 1.0)
    real_part = jnp.clip(real_part, -2.5, 2.5)
    imag_part = jnp.clip(imag_part, -2.5, -0.01)
    return jnp.stack([real_part, imag_part], axis=2)


def place_ends(values, rng, least, top_value):
    dims = values.shape
    place = [jax.random.randint(jax.random.fold_in(rng, axis), (), 0, dims[axis]) for axis in range(len(dims))]
    values = values.at[tuple(place)].set(least)
    longest = dims.index(max(dims))
    place[longest] = (place[longest] + 1) % dims[longest]
    return values.at[tuple(place)].set(top_value)


def steps_of(stream_key, dims, pieces, smallest, largest):
    loudness = 1.0
    for position, parts in pieces:
        draws = jax.random.uniform(jax.random.fold_in(jax.random.fold_in(stream_key, 6), position), (parts,), jnp.float32, smallest / len(pieces), largest / len(pieces))
        loudness = loudness * jnp.repeat(jnp.exp(draws), dims[position] // parts).reshape((-1,) + (1,) * (len(dims) - 1 - position))
    return loudness


def centred(own_key, extent, spread, most, split=(), kind=jnp.bfloat16):
    loudness = steps_of(own_key, extent, split, -0.22, 0.18) if split else 1.0
    entries = jax.random.normal(own_key, extent, jnp.float32) * spread * loudness
    return jnp.minimum(jnp.maximum(entries, -most), most).astype(kind)


def setup_inputs(seed: int = 0) -> dict:
    key_list = jax.random.split(jax.random.key(seed), 7)
    hamiltonian = draw_hamiltonian(jax.random.fold_in(key_list[6], 71), 0)
    coupling = centred(key_list[1], (SLABS, NO, NO), NO ** -0.5, 0.5, ((0, 2),), jnp.float32)
    bonds = place_ends((jax.random.randint(key_list[2], (SLABS, NO), 0, 4) < 3).astype(jnp.int32), jax.random.fold_in(key_list[2], 1), 0, 1)
    phonon_coupling = jnp.clip(jnp.exp(math.log(1.0) - 2.3025851 * jax.random.uniform(key_list[3], (SLABS, NO), jnp.float32) ** steps_of(key_list[3], (SLABS, NO), ((0, 2),), -0.2, 0.2)), 0.1, 1.0)
    previous_green = draw_previous_green(jax.random.fold_in(key_list[6], 71), 0)
    phonon_shift = place_ends(jax.random.randint(key_list[5], (SLABS,), 1, ENER_DEV + 1), jax.random.fold_in(key_list[5], 1), 1, ENER_DEV).astype(jnp.int32)
    return {"hamiltonian": hamiltonian, "coupling": coupling, "bonds": bonds, "phonon_coupling": phonon_coupling, "previous_green": previous_green, "phonon_shift": phonon_shift}


HIGHEST = lax.Precision.HIGHEST
BROADENING = 0.2
LEAD_WIDTH = 0.5
THERMAL = 0.1
HALF_WINDOW = 3.0

def product(left, right):
    return jnp.matmul(left, right, precision=HIGHEST)

def chol_apply(factor, right_side):
    inner = lax.linalg.triangular_solve(factor, right_side, left_side=True, lower=True)
    return lax.linalg.triangular_solve(factor, inner, left_side=True, lower=True, transpose_a=True)

def invert(blocks):
    real_part = blocks[:, 0]
    imag_part = blocks[:, 1]
    lower_imag = jnp.linalg.cholesky(imag_part)
    ratio_matrix = chol_apply(lower_imag, real_part)
    schur_block = imag_part + product(real_part, ratio_matrix)
    lower_schur = jnp.linalg.cholesky(schur_block)
    identity = jnp.broadcast_to(jnp.eye(schur_block.shape[-1], dtype=schur_block.dtype), schur_block.shape)
    imag_inverse = -chol_apply(lower_schur, identity)
    real_inverse = -product(ratio_matrix, imag_inverse)
    return jnp.stack([real_inverse, imag_inverse], axis=1)

def project_left(weight, blocks):
    return product(product(weight.T, blocks), weight)

def project_right(weight, blocks):
    return product(product(weight, blocks), weight.T)

def slab_matrix(hamiltonian_block, phonon_self, energy_grid):
    identity = jnp.eye(hamiltonian_block.shape[0], dtype=jnp.float32)
    real_part = energy_grid[:, None, None] * identity - hamiltonian_block - phonon_self[:, 0, None, :] * identity
    imag_part = BROADENING * identity - phonon_self[:, 1, None, :] * identity
    return jnp.stack([real_part, imag_part], axis=1)

def reference(hamiltonian, coupling, bonds, phonon_coupling, previous_green, phonon_shift):
    orbitals = hamiltonian.shape[1]
    energy_grid = -HALF_WINDOW + 2.0 * HALF_WINDOW * (jnp.arange(ENERGIES, dtype=jnp.int32).astype(jnp.float32) + 0.5) / ENERGIES
    padded = jnp.pad(previous_green, ((ENER_DEV, ENER_DEV), (0, 0), (0, 0), (0, 0)))
    weights = coupling * bonds[:, None, :].astype(jnp.float32)
    identity = jnp.eye(orbitals, dtype=jnp.float32)
    zeros_block = jnp.zeros_like(identity)

    def matrices_of(slab_index):
        shift_steps = phonon_shift[slab_index].astype(jnp.int32)
        column = padded[:, slab_index]
        below_shift = lax.dynamic_slice_in_dim(column, (ENER_DEV - shift_steps).astype(jnp.int32), ENERGIES, 0)
        above_shift = lax.dynamic_slice_in_dim(column, (ENER_DEV + shift_steps).astype(jnp.int32), ENERGIES, 0)
        phonon_self = phonon_coupling[slab_index] * (below_shift + above_shift)
        return slab_matrix(hamiltonian[slab_index], phonon_self, energy_grid)
    carried = jnp.broadcast_to(jnp.stack([zeros_block, -identity]), (ENERGIES, 2, orbitals, orbitals))
    left_selves = []
    for slab_index in range(SLABS):
        self_left = project_left(weights[slab_index], carried)
        left_selves.append(self_left)
        carried = invert(matrices_of(slab_index) - self_left)
    carried = jnp.broadcast_to(jnp.stack([zeros_block, -LEAD_WIDTH * identity]), (ENERGIES, 2, orbitals, orbitals))
    green_list = [None] * SLABS
    for slab_index in reversed(range(SLABS)):
        matrix_now = matrices_of(slab_index)
        green_list[slab_index] = invert(matrix_now - left_selves[slab_index] - carried)
        carried = project_right(weights[slab_index], invert(matrix_now - carried))
    green_blocks = jnp.stack(green_list, axis=1)
    occupation = jax.nn.sigmoid(-energy_grid / THERMAL)
    diagonal = jnp.diagonal(green_blocks[:, :, 1], axis1=-2, axis2=-1)
    summed = jnp.sum(occupation[:, None, None] * diagonal, axis=0)
    density = -2.0 * HALF_WINDOW / ENERGIES / jnp.pi * summed
    return (green_blocks, density)
```

```python
import functools

import jax
import jax.numpy as jnp
from jax import lax
from jax.experimental import pallas as pl
from jax.experimental.pallas import tpu as pltpu
from jax.sharding import Mesh
from jax.sharding import PartitionSpec as P

ENERGY = ("energy_0", "energy_1", "energy_2")
BROADENING = 0.2
LEAD_WIDTH = 0.5
THERMAL = 0.1
HALF_WINDOW = 3.0
GROUP = 8
PANEL = 32
ROWS = (((0,), (0,)), ((), ()))
PLAIN = (((1,), (0,)), ((), ()))
COLUMNS = (((1,), (1,)), ((), ()))
VMEM = pl.BlockSpec(memory_space=pltpu.VMEM)
SMEM = pl.BlockSpec(memory_space=pltpu.SMEM)


def split(x):
    high = x.astype(jnp.bfloat16)
    return high, (x - high.astype(jnp.float32)).astype(jnp.bfloat16)


def dot(left, right, dims=PLAIN):
    return lax.dot_general(left, right, dims, preferred_element_type=jnp.float32)


def product(left, right, dims=PLAIN):
    (lh, ll), (rh, rl) = split(left), split(right)
    return dot(lh, rh, dims) + (dot(ll, rh, dims) + dot(lh, rl, dims))


def eye(n):
    return lax.broadcasted_iota(jnp.int32, (n, n), 0) == lax.broadcasted_iota(jnp.int32, (n, n), 1)


def eliminate(rows, first):
    count, width = len(rows), rows[0][0].shape[1]
    lane = lax.broadcasted_iota(jnp.int32, (GROUP, width), 1)
    row = lax.broadcasted_iota(jnp.int32, (GROUP, width), 0)

    def column(x, j):
        return jnp.broadcast_to(jnp.sum(jnp.where(lane == j, x, 0.0), axis=1, keepdims=True), x.shape)

    def spread(x, k):
        return jnp.broadcast_to(x[k : k + 1, :], x.shape)

    for g in range(count):
        start = first + g * GROUP
        order = [(g + t) % count for t in range(count)]
        columns = {h: [(column(rows[h][0], start + k), column(rows[h][1], start + k)) for k in range(GROUP)] for h in order}
        pivots = list(columns[g])
        inside = (lane >= start) & (lane < start + GROUP)
        xr = jnp.where(inside, jnp.where(lane == start + row, 1.0, 0.0), rows[g][0])
        xi = jnp.where(inside, 0.0, rows[g][1])
        for k in range(GROUP):
            cr, ci = pivots[k]
            pr, pi = spread(cr, k), spread(ci, k)
            d = 1.0 / (pr * pr + pi * pi)
            qr, qi = pr * d, -(pi * d)
            wr = jnp.where(row == k, 1.0 - qr, cr * qr - ci * qi)
            wi = jnp.where(row == k, -qi, cr * qi + ci * qr)
            for j in range(k + 1, GROUP):
                sr, si = spread(pivots[j][0], k), spread(pivots[j][1], k)
                pivots[j] = (pivots[j][0] - (wr * sr - wi * si), pivots[j][1] - (wr * si + wi * sr))
            sr, si = spread(xr, k), spread(xi, k)
            xr, xi = xr - (wr * sr - wi * si), xi - (wr * si + wi * sr)
        rows[g] = (xr, xi)
        for h in order[1:]:
            yr, yi = jnp.where(inside, 0.0, rows[h][0]), jnp.where(inside, 0.0, rows[h][1])
            for k in range(GROUP):
                cr, ci = columns[h][k]
                sr, si = spread(xr, k), spread(xi, k)
                yr, yi = yr - (cr * sr - ci * si), yi - (cr * si + ci * sr)
            rows[h] = (yr, yi)
    return rows


def invert(real, imag):
    energies, n = real.shape[0], real.shape[-1]
    lane = lax.broadcasted_iota(jnp.int32, (PANEL, n), 1)
    for first in range(0, n, PANEL):
        inside = (lane >= first) & (lane < first + PANEL)
        for e in range(energies):
            before = jnp.concatenate([real[e, first : first + PANEL, :], imag[e, first : first + PANEL, :]], axis=0)
            rows = []
            for at in range(first, first + PANEL, GROUP):
                rows.append((real[e, at : at + GROUP, :], imag[e, at : at + GROUP, :]))
            rows = eliminate(rows, first)
            tr = jnp.concatenate([x for x, _ in rows], axis=0)
            ti = jnp.concatenate([y for _, y in rows], axis=0)
            tr, ti = jnp.where(inside, -tr, tr), jnp.where(inside, -ti, ti)
            after = jnp.concatenate(
                [jnp.concatenate([tr, ti], axis=1), jnp.concatenate([-ti, tr], axis=1)], axis=0
            )
            (lh, ll), (rh, rl) = split(before), split(after)
            update = dot(
                jnp.concatenate([lh, ll, lh, ll], axis=0), jnp.concatenate([rh, rh, rl, rl], axis=0), ROWS
            )
            for at in range(0, n, PANEL):
                s = slice(at, at + PANEL)
                if at == first:
                    real[e, s, :], imag[e, s, :] = tr, ti
                else:
                    real[e, s, :] = jnp.where(inside, 0.0, real[e, s, :]) - update[s, :n]
                    imag[e, s, :] = jnp.where(inside, 0.0, imag[e, s, :]) - update[s, n:]


def pair(real, imag):
    return jnp.concatenate(
        [jnp.concatenate([real, imag], axis=1), jnp.concatenate([-imag, real], axis=1)], axis=0
    )


def chain(role, shifts, grid, ham, weights, strength, own, before, after, outer_x, outer_t, inner_s, inner_x, real, imag):
    energies, n = own.shape[0], ham.shape[-1]
    rank = role[0]
    diagonal = eye(n)

    def build(slab):
        one = shifts[slab] == 1
        around = [before.at[e] for e in range(energies)] + [own.at[e] for e in range(energies)]
        around += [after.at[e] for e in range(energies)]
        blocks = []
        for e in range(energies):
            at = [around[energies + e + step][slab] for step in (-2, -1, 1, 2)]
            green = jnp.where(one, at[1] + at[2], at[0] + at[3])
            self_energy = strength[pl.ds(slab, 1), :] * green
            re = jnp.where(diagonal, grid[e] - self_energy[0:1, :], 0.0) - ham[slab]
            im = jnp.where(diagonal, BROADENING - self_energy[1:2, :], 0.0)
            blocks.append((re, im))
        return blocks

    w_near = weights[0]
    v = weights[1]
    v = jnp.where(rank == 0, v, v.T)
    lead = jnp.where(rank == 0, product(w_near, w_near, ROWS), jnp.where(diagonal, LEAD_WIDTH, 0.0))
    for e, (re, im) in enumerate(build(rank)):
        real[e] = re
        imag[e] = im + lead
    invert(real, imag)
    inner = build(1 - rank)
    for e in range(energies):
        xr, xi = -real[e], -imag[e]
        outer_x[e, 0] = xr
        outer_x[e, 1] = xi
        t = product(jnp.concatenate([xr, xi], axis=0), v)
        tr, ti = t[:n], t[n:]
        outer_t[e, 0] = tr
        outer_t[e, 1] = ti
        self_energy = product(v, jnp.concatenate([tr, ti], axis=1), ROWS)
        re = inner[e][0] - self_energy[:, :n]
        im = inner[e][1] - self_energy[:, n:]
        inner_s[e, 0] = re
        inner_s[e, 1] = im
        real[e] = re
        imag[e] = im
    invert(real, imag)
    for e in range(energies):
        inner_x[e, 0] = -real[e]
        inner_x[e, 1] = -imag[e]


def close(role, occupation, outer_x, outer_t, inner_s, received, w, green, density, real, imag):
    energies, n = outer_x.shape[0], w.shape[-1]
    rank = role[0]
    diagonal = eye(n)
    u = w[...]
    u = jnp.where(rank == 0, u.T, u)
    for e in range(energies):
        t = product(jnp.concatenate([received[e, 0], received[e, 1]], axis=0), u)
        self_energy = product(u, jnp.concatenate([t[:n], t[n:]], axis=1), ROWS)
        real[e] = inner_s[e, 0] - self_energy[:, :n]
        imag[e] = inner_s[e, 1] - self_energy[:, n:]
    invert(real, imag)
    inner_sum = jnp.zeros((1, n), jnp.float32)
    outer_sum = jnp.zeros((1, n), jnp.float32)
    for e in range(energies):
        gr, gi = -real[e], -imag[e]
        green[e, 1 - rank, 0] = gr
        green[e, 1 - rank, 1] = gi
        tr, ti = outer_t[e, 0], outer_t[e, 1]
        y = product(jnp.concatenate([tr, ti], axis=1), pair(gr, gi))
        z = product(y, jnp.concatenate([jnp.concatenate([tr, -ti], axis=1), jnp.concatenate([ti, tr], axis=1)], axis=0), COLUMNS)
        or_, oi = outer_x[e, 0] + z[:, :n], outer_x[e, 1] + z[:, n:]
        green[e, rank, 0] = or_
        green[e, rank, 1] = oi
        inner_sum += occupation[e] * jnp.sum(jnp.where(diagonal, gi, 0.0), axis=0, keepdims=True)
        outer_sum += occupation[e] * jnp.sum(jnp.where(diagonal, oi, 0.0), axis=0, keepdims=True)
    density[pl.ds(rank, 1), :] = outer_sum
    density[pl.ds(1 - rank, 1), :] = inner_sum


def exchange(x):
    return lax.ppermute(x, "slab", [(0, 1), (1, 0)])


def shards(hamiltonian, coupling, bonds, phonon_coupling, previous_green, phonon_shift):
    energies, n = previous_green.shape[0], hamiltonian.shape[1]
    rank = lax.axis_index("slab")
    size = lax.axis_size(ENERGY)
    total = energies * size
    first = lax.axis_index(ENERGY) * energies
    points = (jnp.arange(energies, dtype=jnp.int32) + first).astype(jnp.float32) + 0.5
    grid = -HALF_WINDOW + 2.0 * HALF_WINDOW * points / total
    up = [(i, i + 1) for i in range(size - 1)]
    before = lax.ppermute(previous_green, ENERGY, up)
    after = lax.ppermute(previous_green, ENERGY, [(j, i) for i, j in up])
    weights = coupling * bonds[:, None, :].astype(jnp.float32)
    theirs = exchange(weights[0])
    middle = jnp.where(rank == 0, theirs, weights[0])
    role = jnp.reshape(rank, (1,)).astype(jnp.int32)
    block = jax.ShapeDtypeStruct((energies, 2, n, n), jnp.float32)
    scratch = [pltpu.VMEM((energies, n, n), jnp.float32)] * 2
    outer_x, outer_t, inner_s, inner_x = pl.pallas_call(
        chain,
        out_shape=[block] * 4,
        in_specs=[SMEM] * 3 + [VMEM] * 6,
        out_specs=[VMEM] * 4,
        scratch_shapes=scratch,
        name="chain",
    )(role, phonon_shift, grid, hamiltonian, weights, phonon_coupling, previous_green, before, after)
    received = exchange(inner_x)
    green, partial = pl.pallas_call(
        close,
        out_shape=[
            jax.ShapeDtypeStruct((energies, 2, 2, n, n), jnp.float32),
            jax.ShapeDtypeStruct((2, n), jnp.float32),
        ],
        in_specs=[SMEM] * 2 + [VMEM] * 5,
        out_specs=[VMEM] * 2,
        scratch_shapes=scratch,
        name="close",
    )(role, jax.nn.sigmoid(-grid / THERMAL), outer_x, outer_t, inner_s, received, middle)
    summed = functools.reduce(lax.psum, ENERGY, partial)
    return green, -2.0 * HALF_WINDOW / total / jnp.pi * summed


def solution(mesh):
    split_mesh = Mesh(mesh.devices.reshape(8, 8, 4, mesh.shape["slab"]), (*ENERGY, "slab"))
    in_specs = (
        P("slab", None, None),
        P("slab", None, None),
        P("slab", None),
        P("slab", None),
        P(ENERGY, "slab", None, None),
        P("slab"),
    )
    out_specs = (P(ENERGY, "slab", None, None, None), P("slab", None))
    return jax.shard_map(shards, mesh=split_mesh, in_specs=in_specs, out_specs=out_specs, check_vma=False)
```

```python
import functools

import jax
import jax.numpy as jnp
from jax import lax
from jax.experimental import pallas as pl
from jax.experimental.pallas import tpu as pltpu
from jax.sharding import Mesh
from jax.sharding import PartitionSpec as P

ENERGY = ("energy_0", "energy_1", "energy_2")
MESH = pl.DeviceIdType.MESH
BROADENING = 0.2
LEAD_WIDTH = 0.5
THERMAL = 0.1
HALF_WINDOW = 3.0
GROUP = 8
PANEL = 32
ROWS = (((0,), (0,)), ((), ()))
PLAIN = (((1,), (0,)), ((), ()))
COLUMNS = (((1,), (1,)), ((), ()))
VMEM = pl.BlockSpec(memory_space=pltpu.VMEM)
SMEM = pl.BlockSpec(memory_space=pltpu.SMEM)


def split(x):
    high = x.astype(jnp.bfloat16)
    return high, (x - high.astype(jnp.float32)).astype(jnp.bfloat16)


def dot(left, right, dims=PLAIN):
    return lax.dot_general(left, right, dims, preferred_element_type=jnp.float32)


def product(left, right, dims=PLAIN):
    (lh, ll), (rh, rl) = split(left), split(right)
    return dot(lh, rh, dims) + (dot(ll, rh, dims) + dot(lh, rl, dims))


def eye(n):
    return lax.broadcasted_iota(jnp.int32, (n, n), 0) == lax.broadcasted_iota(jnp.int32, (n, n), 1)


def eliminate(rows, first):
    count, width = len(rows), rows[0][0].shape[1]
    lane = lax.broadcasted_iota(jnp.int32, (GROUP, width), 1)
    row = lax.broadcasted_iota(jnp.int32, (GROUP, width), 0)

    def column(x, j):
        return jnp.broadcast_to(jnp.sum(jnp.where(lane == j, x, 0.0), axis=1, keepdims=True), x.shape)

    def spread(x, k):
        return jnp.broadcast_to(x[k : k + 1, :], x.shape)

    for g in range(count):
        start = first + g * GROUP
        order = [(g + t) % count for t in range(count)]
        columns = {h: [(column(rows[h][0], start + k), column(rows[h][1], start + k)) for k in range(GROUP)] for h in order}
        pivots = list(columns[g])
        inside = (lane >= start) & (lane < start + GROUP)
        xr = jnp.where(inside, jnp.where(lane == start + row, 1.0, 0.0), rows[g][0])
        xi = jnp.where(inside, 0.0, rows[g][1])
        for k in range(GROUP):
            cr, ci = pivots[k]
            pr, pi = spread(cr, k), spread(ci, k)
            d = 1.0 / (pr * pr + pi * pi)
            qr, qi = pr * d, -(pi * d)
            wr = jnp.where(row == k, 1.0 - qr, cr * qr - ci * qi)
            wi = jnp.where(row == k, -qi, cr * qi + ci * qr)
            for j in range(k + 1, GROUP):
                sr, si = spread(pivots[j][0], k), spread(pivots[j][1], k)
                pivots[j] = (pivots[j][0] - (wr * sr - wi * si), pivots[j][1] - (wr * si + wi * sr))
            sr, si = spread(xr, k), spread(xi, k)
            xr, xi = xr - (wr * sr - wi * si), xi - (wr * si + wi * sr)
        rows[g] = (xr, xi)
        for h in order[1:]:
            yr, yi = jnp.where(inside, 0.0, rows[h][0]), jnp.where(inside, 0.0, rows[h][1])
            for k in range(GROUP):
                cr, ci = columns[h][k]
                sr, si = spread(xr, k), spread(xi, k)
                yr, yi = yr - (cr * sr - ci * si), yi - (cr * si + ci * sr)
            rows[h] = (yr, yi)
    return rows


def invert(real, imag):
    energies, n = real.shape[0], real.shape[-1]
    lane = lax.broadcasted_iota(jnp.int32, (PANEL, n), 1)
    for first in range(0, n, PANEL):
        inside = (lane >= first) & (lane < first + PANEL)
        for e in range(energies):
            before = jnp.concatenate([real[e, first : first + PANEL, :], imag[e, first : first + PANEL, :]], axis=0)
            rows = []
            for at in range(first, first + PANEL, GROUP):
                rows.append((real[e, at : at + GROUP, :], imag[e, at : at + GROUP, :]))
            rows = eliminate(rows, first)
            tr = jnp.concatenate([x for x, _ in rows], axis=0)
            ti = jnp.concatenate([y for _, y in rows], axis=0)
            tr, ti = jnp.where(inside, -tr, tr), jnp.where(inside, -ti, ti)
            after = jnp.concatenate(
                [jnp.concatenate([tr, ti], axis=1), jnp.concatenate([-ti, tr], axis=1)], axis=0
            )
            (lh, ll), (rh, rl) = split(before), split(after)
            update = dot(
                jnp.concatenate([lh, ll, lh, ll], axis=0), jnp.concatenate([rh, rh, rl, rl], axis=0), ROWS
            )
            for at in range(0, n, PANEL):
                s = slice(at, at + PANEL)
                if at == first:
                    real[e, s, :], imag[e, s, :] = tr, ti
                else:
                    real[e, s, :] = jnp.where(inside, 0.0, real[e, s, :]) - update[s, :n]
                    imag[e, s, :] = jnp.where(inside, 0.0, imag[e, s, :]) - update[s, n:]


def pair(real, imag):
    return jnp.concatenate(
        [jnp.concatenate([real, imag], axis=1), jnp.concatenate([-imag, real], axis=1)], axis=0
    )


def sweep(
    ham, coupling, bonds, strength, shifts, own, green_out, density,
    before, after, near_w, near_b, outer_x, outer_t, inner_s, send_x, recv_x, green, real, imag,
    partials, line_0, line_1, line_2, halo_send, halo_recv, near_send, near_recv, x_send, x_recv,
    line_send, line_recv_0, line_recv_1, line_recv_2, out_sem,
):
    energies, n = own.shape[0], ham.shape[-1]
    rank = lax.axis_index("slab")
    sizes = [lax.axis_size(axis) for axis in ENERGY]
    place = [lax.axis_index(axis) for axis in ENERGY]
    devices = sizes[0] * sizes[1] * sizes[2]
    index = (place[0] * sizes[1] + place[1]) * sizes[2] + place[2]

    def along(step):
        other = lax.rem(index + step, devices)
        return (lax.div(other, sizes[1] * sizes[2]), lax.rem(lax.div(other, sizes[2]), sizes[1]), lax.rem(other, sizes[2]), rank)

    following, previous = along(1), along(devices - 1)
    partner = (*place, 1 - rank)
    lines = [
        [(*place[:a], lax.rem(place[a] + step, sizes[a]), *place[a + 1 :], rank) for step in range(1, sizes[a])]
        for a in range(3)
    ]
    barrier = pltpu.get_barrier_semaphore()
    peers = [following, previous, partner] + lines[0] + lines[1] + lines[2]
    for peer in peers:
        pl.semaphore_signal(barrier, inc=1, device_id=peer, device_id_type=MESH)

    diagonal = eye(n)
    w_near = coupling[0] * bonds[0:1, :].astype(jnp.float32)
    v = coupling[1] * bonds[1:2, :].astype(jnp.float32)
    v = jnp.where(rank == 0, v, v.T)
    lead = jnp.where(rank == 0, product(w_near, w_near, ROWS), jnp.where(diagonal, LEAD_WIDTH, 0.0))
    pl.semaphore_wait(barrier, len(peers))

    def remote(source, target, send, recv, device):
        return pltpu.make_async_remote_copy(source, target, send, recv, device_id=device, device_id_type=MESH)

    halo = [
        remote(own, before, halo_send.at[0], halo_recv.at[0], following),
        remote(own, after, halo_send.at[1], halo_recv.at[1], previous),
    ]
    near = [
        remote(coupling.at[0], near_w, near_send.at[0], near_recv.at[0], partner),
        remote(bonds, near_b, near_send.at[1], near_recv.at[1], partner),
    ]
    for copy in halo + near:
        copy.start()
    for copy in halo:
        copy.wait()

    points = [
        -HALF_WINDOW + 2.0 * HALF_WINDOW * ((index * energies + e).astype(jnp.float32) + 0.5) / (devices * energies)
        for e in range(energies)
    ]
    has_before, has_after = index > 0, index < devices - 1

    def build(slab):
        one = shifts[slab] == 1
        around = [jnp.where(has_before, before[e, slab], 0.0) for e in range(energies)]
        around += [own[e, slab] for e in range(energies)]
        around += [jnp.where(has_after, after[e, slab], 0.0) for e in range(energies)]
        blocks = []
        for e in range(energies):
            far, close, close_up, far_up = [around[energies + e + step] for step in (-2, -1, 1, 2)]
            self_energy = strength[pl.ds(slab, 1), :] * jnp.where(one, close + close_up, far + far_up)
            re = jnp.where(diagonal, points[e] - self_energy[0:1, :], 0.0) - ham[slab]
            im = jnp.where(diagonal, BROADENING - self_energy[1:2, :], 0.0)
            blocks.append((re, im))
        return blocks

    for e, (re, im) in enumerate(build(rank)):
        real[e] = re
        imag[e] = im + lead
    invert(real, imag)
    inner = build(1 - rank)
    for e in range(energies):
        xr, xi = -real[e], -imag[e]
        outer_x[e, 0] = xr
        outer_x[e, 1] = xi
        t = product(jnp.concatenate([xr, xi], axis=0), v)
        tr, ti = t[:n], t[n:]
        outer_t[e, 0] = tr
        outer_t[e, 1] = ti
        self_energy = product(v, jnp.concatenate([tr, ti], axis=1), ROWS)
        re = inner[e][0] - self_energy[:, :n]
        im = inner[e][1] - self_energy[:, n:]
        inner_s[e, 0] = re
        inner_s[e, 1] = im
        real[e] = re
        imag[e] = im
    invert(real, imag)
    for e in range(energies):
        send_x[e, 0] = -real[e]
        send_x[e, 1] = -imag[e]
    swap = remote(send_x, recv_x, x_send.at[0], x_recv.at[0], partner)
    swap.start()
    for copy in near:
        copy.wait()
    theirs = near_w[...] * near_b[0:1, :].astype(jnp.float32)
    u = jnp.where(rank == 0, theirs.T, w_near)
    swap.wait()
    for e in range(energies):
        t = product(jnp.concatenate([recv_x[e, 0], recv_x[e, 1]], axis=0), u)
        self_energy = product(u, jnp.concatenate([t[:n], t[n:]], axis=1), ROWS)
        real[e] = inner_s[e, 0] - self_energy[:, :n]
        imag[e] = inner_s[e, 1] - self_energy[:, n:]
    invert(real, imag)
    inner_sum = jnp.zeros((1, n), jnp.float32)
    outer_sum = jnp.zeros((1, n), jnp.float32)
    stores = []
    for e in range(energies):
        gr, gi = -real[e], -imag[e]
        green[e, 1 - rank, 0] = gr
        green[e, 1 - rank, 1] = gi
        tr, ti = outer_t[e, 0], outer_t[e, 1]
        y = product(jnp.concatenate([tr, ti], axis=1), pair(gr, gi))
        turned = jnp.concatenate([jnp.concatenate([tr, -ti], axis=1), jnp.concatenate([ti, tr], axis=1)], axis=0)
        z = product(y, turned, COLUMNS)
        re, im = outer_x[e, 0] + z[:, :n], outer_x[e, 1] + z[:, n:]
        green[e, rank, 0] = re
        green[e, rank, 1] = im
        occupied = 1.0 / (1.0 + jnp.exp(jnp.full((1, n), points[e] / THERMAL, jnp.float32)))
        inner_sum += occupied * jnp.sum(jnp.where(diagonal, gi, 0.0), axis=0, keepdims=True)
        outer_sum += occupied * jnp.sum(jnp.where(diagonal, im, 0.0), axis=0, keepdims=True)
    partials[0, pl.ds(rank, 1), :] = outer_sum
    partials[0, pl.ds(1 - rank, 1), :] = inner_sum
    store = pltpu.make_async_copy(green, green_out, out_sem.at[0])
    store.start()
    buffers = [line_0, line_1, line_2]
    arrivals = [line_recv_0, line_recv_1, line_recv_2]
    for stage, a in enumerate((2, 1, 0)):
        buffer, arrival, mine = buffers[a], arrivals[a], place[a]
        source = partials.at[stage]
        copies = [
            remote(source, buffer.at[mine], line_send.at[a, step], arrival.at[mine], device)
            for step, device in enumerate(lines[a])
        ]
        for copy in copies:
            copy.start()
        buffer[mine] = partials[stage]
        for step in range(1, sizes[a]):
            sender = lax.rem(mine + step, sizes[a])
            remote(source, buffer.at[sender], line_send.at[a, step - 1], arrival.at[sender], lines[a][step - 1]).wait_recv()
        total = buffer[0]
        for other in range(1, sizes[a]):
            total = total + buffer[other]
        if stage < 2:
            partials[stage + 1] = total
        else:
            density[...] = (-2.0 * HALF_WINDOW / (devices * energies) / jnp.pi) * total
        for copy in copies:
            copy.wait_send()
    store.wait()


def shards(hamiltonian, coupling, bonds, phonon_coupling, previous_green, phonon_shift):
    energies, slabs, n = previous_green.shape[0], hamiltonian.shape[0], hamiltonian.shape[1]
    sizes = [lax.axis_size(axis) for axis in ENERGY]
    longest = max(sizes)
    block = pltpu.VMEM((energies, 2, n, n), jnp.float32)
    square = pltpu.VMEM((energies, n, n), jnp.float32)
    halo = pltpu.VMEM(previous_green.shape, jnp.float32)
    dma = pltpu.SemaphoreType.DMA
    return pl.pallas_call(
        sweep,
        out_shape=(
            jax.ShapeDtypeStruct((energies, slabs, 2, n, n), jnp.float32),
            jax.ShapeDtypeStruct((slabs, n), jnp.float32),
        ),
        in_specs=[VMEM] * 4 + [SMEM, VMEM],
        out_specs=(pl.BlockSpec(memory_space=pl.ANY), VMEM),
        scratch_shapes=[
            halo, halo, pltpu.VMEM((n, n), jnp.float32), pltpu.VMEM(bonds.shape, jnp.int32),
            block, block, block, block, block, pltpu.VMEM((energies, slabs, 2, n, n), jnp.float32), square, square,
            pltpu.VMEM((3, slabs, n), jnp.float32),
            *[pltpu.VMEM((size, slabs, n), jnp.float32) for size in sizes],
            dma((2,)), dma((2,)), dma((2,)), dma((2,)), dma((1,)), dma((1,)),
            dma((3, longest)), *[dma((size,)) for size in sizes], dma((1,)),
        ],
        compiler_params=pltpu.CompilerParams(collective_id=0, has_side_effects=True),
        name="sweep",
    )(hamiltonian, coupling, bonds, phonon_coupling, phonon_shift, previous_green)


def solution(mesh):
    split_mesh = Mesh(mesh.devices.reshape(8, 8, 4, mesh.shape["slab"]), (*ENERGY, "slab"))
    in_specs = (
        P("slab", None, None),
        P("slab", None, None),
        P("slab", None),
        P("slab", None),
        P(ENERGY, "slab", None, None),
        P("slab"),
    )
    out_specs = (P(ENERGY, "slab", None, None, None), P("slab", None))
    return jax.shard_map(shards, mesh=split_mesh, in_specs=in_specs, out_specs=out_specs, check_vma=False)
```

```python
import functools

import jax
import jax.numpy as jnp
from jax import lax
from jax.experimental import pallas as pl
from jax.experimental.pallas import tpu as pltpu
from jax.sharding import Mesh
from jax.sharding import PartitionSpec as P

ENERGY = ("energy_0", "energy_1", "energy_2")
MESH = pl.DeviceIdType.MESH
BROADENING = 0.2
LEAD_WIDTH = 0.5
THERMAL = 0.1
HALF_WINDOW = 3.0
GROUP = 8
PANEL = 16
ROWS = (((0,), (0,)), ((), ()))
PLAIN = (((1,), (0,)), ((), ()))
COLUMNS = (((1,), (1,)), ((), ()))
VMEM = pl.BlockSpec(memory_space=pltpu.VMEM)
HBM = pl.BlockSpec(memory_space=pltpu.HBM)


def split(x):
    high = x.astype(jnp.bfloat16)
    return high, (x - high.astype(jnp.float32)).astype(jnp.bfloat16)


def dot(left, right, dims=PLAIN):
    return lax.dot_general(left, right, dims, preferred_element_type=jnp.float32)


def product(left, right, dims=PLAIN):
    (lh, ll), (rh, rl) = split(left), split(right)
    return dot(lh, rh, dims) + (dot(ll, rh, dims) + dot(lh, rl, dims))


def eye(n):
    return lax.broadcasted_iota(jnp.int32, (n, n), 0) == lax.broadcasted_iota(jnp.int32, (n, n), 1)


def times(a, b):
    return a[0] * b[0] - a[1] * b[1], a[0] * b[1] + a[1] * b[0]


def minus(a, b):
    return a[0] - b[0], a[1] - b[1]


def spread(x, k):
    return tuple(jnp.broadcast_to(part[k : k + 1, :], part.shape) for part in x)


def total_of(parts):
    while len(parts) > 1:
        parts = [parts[i] + parts[i + 1] for i in range(0, len(parts), 2)]
    return parts[0]


def eliminate(panels, first):
    energies, count = range(len(panels)), len(panels[0])
    shape = panels[0][0][0].shape
    lane = lax.broadcasted_iota(jnp.int32, shape, 1)
    row = lax.broadcasted_iota(jnp.int32, shape, 0)

    def column(x, j):
        return tuple(
            jnp.broadcast_to(jnp.sum(jnp.where(lane == j, part, 0.0), axis=1, keepdims=True), shape) for part in x
        )

    for g in range(count):
        start = first + g * GROUP
        inside = (lane >= start) & (lane < start + GROUP)
        unit = jnp.where(lane == start + row, 1.0, 0.0)
        others = [(g + t) % count for t in range(1, count)]
        pivots = [[column(panels[e][g], start + k) for k in range(GROUP)] for e in energies]
        solved = [
            (jnp.where(inside, unit, panels[e][g][0]), jnp.where(inside, 0.0, panels[e][g][1])) for e in energies
        ]
        columns = [{h: [column(panels[e][h], start + k) for k in range(GROUP)] for h in others} for e in energies]
        for k in range(GROUP):
            for e in energies:
                c = pivots[e][k]
                p = spread(c, k)
                d = 1.0 / (p[0] * p[0] + p[1] * p[1])
                q = (p[0] * d, -(p[1] * d))
                w = times(c, q)
                w = (jnp.where(row == k, 1.0 - q[0], w[0]), jnp.where(row == k, -q[1], w[1]))
                for j in range(k + 1, GROUP):
                    pivots[e][j] = minus(pivots[e][j], times(w, spread(pivots[e][j], k)))
                solved[e] = minus(solved[e], times(w, spread(solved[e], k)))
        for e in energies:
            panels[e][g] = solved[e]
            lines = [spread(solved[e], k) for k in range(GROUP)]
            for h in others:
                terms = [times(columns[e][h][k], lines[k]) for k in range(GROUP)]
                rest = tuple(jnp.where(inside, 0.0, part) for part in panels[e][h])
                panels[e][h] = minus(rest, (total_of([t[0] for t in terms]), total_of([t[1] for t in terms])))
    return panels


def invert(real, imag):
    energies, n = real.shape[0], real.shape[-1]
    lane = lax.broadcasted_iota(jnp.int32, (PANEL, n), 1)
    for first in range(0, n, PANEL):
        inside = (lane >= first) & (lane < first + PANEL)
        before, panels = [], []
        for e in range(energies):
            before.append(jnp.concatenate([real[e, first : first + PANEL, :], imag[e, first : first + PANEL, :]], axis=0))
            panels.append(
                [(real[e, at : at + GROUP, :], imag[e, at : at + GROUP, :]) for at in range(first, first + PANEL, GROUP)]
            )
        panels = eliminate(panels, first)
        for e in range(energies):
            tr = jnp.concatenate([x for x, _ in panels[e]], axis=0)
            ti = jnp.concatenate([y for _, y in panels[e]], axis=0)
            tr, ti = jnp.where(inside, -tr, tr), jnp.where(inside, -ti, ti)
            (lh, ll), (rh, rl), (ih, il) = split(before[e]), split(tr), split(ti)
            high, low = pair(rh, ih), pair(rl, il)
            update = dot(
                jnp.concatenate([lh, ll, lh, ll], axis=0), jnp.concatenate([high, high, low, low], axis=0), ROWS
            )
            for at in range(0, n, PANEL):
                s = slice(at, at + PANEL)
                if at == first:
                    real[e, s, :], imag[e, s, :] = tr, ti
                else:
                    real[e, s, :] = jnp.where(inside, 0.0, real[e, s, :]) - update[s, :n]
                    imag[e, s, :] = jnp.where(inside, 0.0, imag[e, s, :]) - update[s, n:]


def pair(real, imag):
    return jnp.concatenate(
        [jnp.concatenate([real, imag], axis=1), jnp.concatenate([-imag, real], axis=1)], axis=0
    )


def sweep(
    ham_in, coupling_in, bonds_in, strength_in, shifts_in, own_in, green, density,
    ham, coupling, bonds, strength, shifts, own, before, after, near_w, near_b, outer_x, outer_u, inner_s, send_x, recv_x, real, imag,
    partials, line_0, line_1, line_2, halo_send, halo_recv, near_send, near_recv, x_send, x_recv,
    line_send, line_recv_0, line_recv_1, line_recv_2, load_sem,
):
    loads = [
        pltpu.make_async_copy(source, target, load_sem.at[i])
        for i, (source, target) in enumerate(
            ((coupling_in, coupling), (bonds_in, bonds), (own_in, own), (strength_in, strength), (shifts_in, shifts), (ham_in, ham))
        )
    ]
    for load in loads:
        load.start()
    energies, n = own.shape[0], ham.shape[-1]
    rank = lax.axis_index("slab")
    sizes = [lax.axis_size(axis) for axis in ENERGY]
    place = [lax.axis_index(axis) for axis in ENERGY]
    devices = sizes[0] * sizes[1] * sizes[2]
    index = (place[0] * sizes[1] + place[1]) * sizes[2] + place[2]

    def along(step):
        other = lax.rem(index + step, devices)
        return (lax.div(other, sizes[1] * sizes[2]), lax.rem(lax.div(other, sizes[2]), sizes[1]), lax.rem(other, sizes[2]), rank)

    following, previous = along(1), along(devices - 1)
    partner = (*place, 1 - rank)
    lines = [
        [(*place[:a], lax.rem(place[a] + step, sizes[a]), *place[a + 1 :], rank) for step in range(1, sizes[a])]
        for a in range(3)
    ]
    barrier = pltpu.get_barrier_semaphore()
    peers = [following, previous, partner] + lines[0] + lines[1] + lines[2]
    for peer in peers:
        pl.semaphore_signal(barrier, inc=1, device_id=peer, device_id_type=MESH)

    diagonal = eye(n)
    for load in loads[:2]:
        load.wait()
    w_near = coupling[0] * bonds[0:1, :].astype(jnp.float32)
    v = coupling[1] * bonds[1:2, :].astype(jnp.float32)
    v = jnp.where(rank == 0, v, v.T)
    lead = jnp.where(rank == 0, product(w_near, w_near, ROWS), jnp.where(diagonal, LEAD_WIDTH, 0.0))
    pl.semaphore_wait(barrier, len(peers))

    def remote(source, target, send, recv, device):
        return pltpu.make_async_remote_copy(source, target, send, recv, device_id=device, device_id_type=MESH)

    halo = [
        remote(own_in, before, halo_send.at[0], halo_recv.at[0], following),
        remote(own_in, after, halo_send.at[1], halo_recv.at[1], previous),
    ]
    near = [
        remote(coupling_in.at[0], near_w, near_send.at[0], near_recv.at[0], partner),
        remote(bonds_in, near_b, near_send.at[1], near_recv.at[1], partner),
    ]
    for copy in halo + near:
        copy.start()
    for load in loads[2:]:
        load.wait()
    for copy in halo:
        copy.wait()

    points = [
        -HALF_WINDOW + 2.0 * HALF_WINDOW * ((index * energies + e).astype(jnp.float32) + 0.5) / (devices * energies)
        for e in range(energies)
    ]
    has_before, has_after = index > 0, index < devices - 1

    def build(slab):
        one = shifts[slab] == 1
        around = [jnp.where(has_before, before[e, slab], 0.0) for e in range(energies)]
        around += [own[e, slab] for e in range(energies)]
        around += [jnp.where(has_after, after[e, slab], 0.0) for e in range(energies)]
        blocks = []
        for e in range(energies):
            far, close, close_up, far_up = [around[energies + e + step] for step in (-2, -1, 1, 2)]
            self_energy = strength[pl.ds(slab, 1), :] * jnp.where(one, close + close_up, far + far_up)
            re = jnp.where(diagonal, points[e] - self_energy[0:1, :], 0.0) - ham[slab]
            im = jnp.where(diagonal, BROADENING - self_energy[1:2, :], 0.0)
            blocks.append((re, im))
        return blocks

    for e, (re, im) in enumerate(build(rank)):
        real[e] = re
        imag[e] = im + lead
    invert(real, imag)
    inner = build(1 - rank)
    for e in range(energies):
        xr, xi = -real[e], -imag[e]
        outer_x[e, 0] = xr
        outer_x[e, 1] = xi
        t = product(v, jnp.concatenate([xr, xi], axis=1), ROWS)
        outer_u[e, 0] = t[:, :n]
        outer_u[e, 1] = t[:, n:]
        self_energy = product(jnp.concatenate([t[:, :n], t[:, n:]], axis=0), v)
        re = inner[e][0] - self_energy[:n]
        im = inner[e][1] - self_energy[n:]
        inner_s[e, 0] = re
        inner_s[e, 1] = im
        real[e] = re
        imag[e] = im
    invert(real, imag)
    for e in range(energies):
        send_x[e, 0] = -real[e]
        send_x[e, 1] = -imag[e]
    swap = remote(send_x, recv_x, x_send.at[0], x_recv.at[0], partner)
    swap.start()
    for copy in near:
        copy.wait()
    theirs = near_w[...] * near_b[0:1, :].astype(jnp.float32)
    u = jnp.where(rank == 0, theirs.T, w_near)
    swap.wait()
    for e in range(energies):
        t = product(jnp.concatenate([recv_x[e, 0], recv_x[e, 1]], axis=0), u)
        self_energy = product(u, jnp.concatenate([t[:n], t[n:]], axis=1), ROWS)
        real[e] = inner_s[e, 0] - self_energy[:, :n]
        imag[e] = inner_s[e, 1] - self_energy[:, n:]
    invert(real, imag)
    sums = [jnp.zeros((1, n), jnp.float32), jnp.zeros((1, n), jnp.float32)]
    halves = []
    for e in range(energies):
        gr, gi = -real[e], -imag[e]
        ur, ui = outer_u[e, 0], outer_u[e, 1]
        y = product(jnp.concatenate([gr, gi], axis=0), jnp.concatenate([ur, ui], axis=1))
        yr, yi = y[:n, :n] - y[n:, n:], y[:n, n:] + y[n:, :n]
        halves.append((yr, yi))
        outer = outer_x[e, 1] * jnp.where(diagonal, 1.0, 0.0) + (ur * yi + ui * yr)
        occupied = 1.0 / (1.0 + jnp.exp(jnp.full((1, n), points[e] / THERMAL, jnp.float32)))
        sums[0] += occupied * jnp.sum(outer, axis=0, keepdims=True)
        sums[1] += occupied * jnp.sum(jnp.where(diagonal, gi, 0.0), axis=0, keepdims=True)
    partials[0, pl.ds(rank, 1), :] = sums[0]
    partials[0, pl.ds(1 - rank, 1), :] = sums[1]

    def finish():
        for e in range(energies):
            green[e, 1 - rank, 0] = -real[e]
            green[e, 1 - rank, 1] = -imag[e]
            yr, yi = halves[e]
            ur, ui = outer_u[e, 0], outer_u[e, 1]
            left = jnp.concatenate([jnp.concatenate([ur, ui], axis=1), jnp.concatenate([-ui, ur], axis=1)], axis=0)
            z = product(left, jnp.concatenate([yr, yi], axis=0), ROWS)
            green[e, rank, 0] = outer_x[e, 0] + z[:n]
            green[e, rank, 1] = outer_x[e, 1] + z[n:]

    buffers = [line_0, line_1, line_2]
    arrivals = [line_recv_0, line_recv_1, line_recv_2]
    for stage, a in enumerate((2, 1, 0)):
        buffer, arrival, mine = buffers[a], arrivals[a], place[a]
        source = partials.at[stage]
        copies = [
            remote(source, buffer.at[mine], line_send.at[a, step], arrival.at[mine], device)
            for step, device in enumerate(lines[a])
        ]
        for copy in copies:
            copy.start()
        buffer[mine] = partials[stage]
        if stage == 0:
            finish()
        for step in range(1, sizes[a]):
            sender = lax.rem(mine + step, sizes[a])
            remote(source, buffer.at[sender], line_send.at[a, step - 1], arrival.at[sender], lines[a][step - 1]).wait_recv()
        total = buffer[0]
        for other in range(1, sizes[a]):
            total = total + buffer[other]
        if stage < 2:
            partials[stage + 1] = total
        else:
            density[...] = (-2.0 * HALF_WINDOW / (devices * energies) / jnp.pi) * total
        for copy in copies:
            copy.wait_send()


def shards(hamiltonian, coupling, bonds, phonon_coupling, previous_green, phonon_shift):
    energies, slabs, n = previous_green.shape[0], hamiltonian.shape[0], hamiltonian.shape[1]
    sizes = [lax.axis_size(axis) for axis in ENERGY]
    longest = max(sizes)
    block = pltpu.VMEM((energies, 2, n, n), jnp.float32)
    square = pltpu.VMEM((energies, n, n), jnp.float32)
    halo = pltpu.VMEM(previous_green.shape, jnp.float32)
    dma = pltpu.SemaphoreType.DMA
    return pl.pallas_call(
        sweep,
        out_shape=(
            jax.ShapeDtypeStruct((energies, slabs, 2, n, n), jnp.float32),
            jax.ShapeDtypeStruct((slabs, n), jnp.float32),
        ),
        in_specs=[HBM] * 6,
        out_specs=(VMEM, VMEM),
        scratch_shapes=[
            *[pltpu.VMEM(x.shape, x.dtype) for x in (hamiltonian, coupling, bonds, phonon_coupling)],
            pltpu.SMEM(phonon_shift.shape, jnp.int32), halo, halo, halo, pltpu.VMEM((n, n), jnp.float32), pltpu.VMEM(bonds.shape, jnp.int32),
            block, block, block, block, block, square, square,
            pltpu.VMEM((3, slabs, n), jnp.float32),
            *[pltpu.VMEM((size, slabs, n), jnp.float32) for size in sizes],
            dma((2,)), dma((2,)), dma((2,)), dma((2,)), dma((1,)), dma((1,)),
            dma((3, longest)), *[dma((size,)) for size in sizes], dma((6,)),
        ],
        compiler_params=pltpu.CompilerParams(collective_id=0, has_side_effects=True, vmem_limit_bytes=16 << 20),
        name="sweep",
    )(*[
        pltpu.with_memory_space_constraint(x, pltpu.HBM)
        for x in (hamiltonian, coupling, bonds, phonon_coupling, phonon_shift, previous_green)
    ])


def solution(mesh):
    split_mesh = Mesh(mesh.devices.reshape(8, 8, 4, mesh.shape["slab"]), (*ENERGY, "slab"))
    in_specs = (
        P("slab", None, None),
        P("slab", None, None),
        P("slab", None),
        P("slab", None),
        P(ENERGY, "slab", None, None),
        P("slab"),
    )
    out_specs = (P(ENERGY, "slab", None, None, None), P("slab", None))
    return jax.shard_map(shards, mesh=split_mesh, in_specs=in_specs, out_specs=out_specs, check_vma=False)
```

```python
import functools

import jax
import jax.numpy as jnp
from jax import lax
from jax.experimental import pallas as pl
from jax.experimental.pallas import tpu as pltpu
from jax.sharding import Mesh
from jax.sharding import PartitionSpec as P

ENERGY = ("energy_0", "energy_1", "energy_2")
MESH = pl.DeviceIdType.MESH
BROADENING = 0.2
LEAD_WIDTH = 0.5
THERMAL = 0.1
HALF_WINDOW = 3.0
GROUP = 8
ROWS = (((0,), (0,)), ((), ()))
PLAIN = (((1,), (0,)), ((), ()))
COLUMNS = (((1,), (1,)), ((), ()))
VMEM = pl.BlockSpec(memory_space=pltpu.VMEM)
HBM = pl.BlockSpec(memory_space=pltpu.HBM)


def split(x):
    high = x.astype(jnp.bfloat16)
    return high, (x - high.astype(jnp.float32)).astype(jnp.bfloat16)


def thirds(x):
    parts = []
    for _ in range(3):
        parts.append(x.astype(jnp.bfloat16))
        x = x - parts[-1].astype(jnp.float32)
    return parts


def dot(left, right, dims=PLAIN):
    return lax.dot_general(left, right, dims, preferred_element_type=jnp.float32)


def product(left, right, dims=PLAIN):
    (lh, ll), (rh, rl) = split(left), split(right)
    return dot(lh, rh, dims) + (dot(ll, rh, dims) + dot(lh, rl, dims))


def eye(n):
    return lax.broadcasted_iota(jnp.int32, (n, n), 0) == lax.broadcasted_iota(jnp.int32, (n, n), 1)


def times(a, b):
    return a[0] * b[0] - a[1] * b[1], a[0] * b[1] + a[1] * b[0]


def minus(a, b):
    return a[0] - b[0], a[1] - b[1]


def spread(x, k):
    return tuple(jnp.broadcast_to(part[k : k + 1, :], part.shape) for part in x)


def total_of(parts):
    while len(parts) > 1:
        parts = [parts[i] + parts[i + 1] for i in range(0, len(parts), 2)]
    return parts[0]


def invert(real, imag):
    energies, n = range(real.shape[0]), real.shape[-1]
    shape = (GROUP, n)
    lane = lax.broadcasted_iota(jnp.int32, shape, 1)
    row = lax.broadcasted_iota(jnp.int32, shape, 0)

    def column(x, j):
        return tuple(
            jnp.broadcast_to(jnp.sum(jnp.where(lane == j, part, 0.0), axis=1, keepdims=True), shape) for part in x
        )

    def load(e, at):
        return real[e, at : at + GROUP, :], imag[e, at : at + GROUP, :]

    current = [load(e, 0) for e in energies]
    for first in range(0, n, GROUP):
        inside = (lane >= first) & (lane < first + GROUP)
        unit = jnp.where(lane == first + row, 1.0, 0.0)
        before = current
        pivots = [[column(before[e], first + k) for k in range(GROUP)] for e in energies]
        solved = [(jnp.where(inside, unit, before[e][0]), jnp.where(inside, 0.0, before[e][1])) for e in energies]
        second = first + GROUP
        if second < n:
            following = [load(e, second) for e in energies]
            columns = [[column(following[e], first + k) for k in range(GROUP)] for e in energies]
        for k in range(GROUP):
            for e in energies:
                c = pivots[e][k]
                p = spread(c, k)
                d = 1.0 / (p[0] * p[0] + p[1] * p[1])
                q = (p[0] * d, -(p[1] * d))
                w = times(c, q)
                w = (jnp.where(row == k, 1.0 - q[0], w[0]), jnp.where(row == k, -q[1], w[1]))
                for j in range(k + 1, GROUP):
                    pivots[e][j] = minus(pivots[e][j], times(w, spread(pivots[e][j], k)))
                solved[e] = minus(solved[e], times(w, spread(solved[e], k)))
        current = []
        for e in energies:
            swept = tuple(jnp.where(inside, -part, part) for part in solved[e])
            if second < n:
                terms = [times(columns[e][k], spread(swept, k)) for k in range(GROUP)]
                rest = tuple(jnp.where(inside, 0.0, part) for part in following[e])
                current.append(minus(rest, (total_of([t[0] for t in terms]), total_of([t[1] for t in terms]))))
            left = thirds(jnp.concatenate(before[e], axis=0))
            right = [pair(x, y) for x, y in zip(thirds(swept[0] + unit), thirds(swept[1]))]
            which = ((0, 0), (1, 0), (2, 0), (0, 1), (1, 1), (0, 2))
            update = dot(
                jnp.concatenate([left[i] for i, _ in which], axis=0),
                jnp.concatenate([right[j] for _, j in which], axis=0),
                ROWS,
            )
            for at in [*range(second + GROUP, n, GROUP), *range(0, first, GROUP)]:
                s = slice(at, at + GROUP)
                real[e, s, :] = real[e, s, :] - update[s, :n]
                imag[e, s, :] = imag[e, s, :] - update[s, n:]
            real[e, first:second, :], imag[e, first:second, :] = swept


def pair(real, imag):
    return jnp.concatenate(
        [jnp.concatenate([real, imag], axis=1), jnp.concatenate([-imag, real], axis=1)], axis=0
    )


def sweep(
    ham_in, coupling_in, bonds_in, strength_in, shifts_in, own_in, green, density,
    ham, coupling, bonds, strength, shifts, own, before, after, near_w, near_b, outer_x, outer_u, inner_s, send_x, recv_x, real, imag,
    partials, line_0, line_1, line_2, halo_send, halo_recv, near_send, near_recv, x_send, x_recv,
    line_send, line_recv_0, line_recv_1, line_recv_2, load_sem,
):
    loads = [
        pltpu.make_async_copy(source, target, load_sem.at[i])
        for i, (source, target) in enumerate(
            ((coupling_in, coupling), (bonds_in, bonds), (own_in, own), (strength_in, strength), (shifts_in, shifts), (ham_in, ham))
        )
    ]
    for load in loads:
        load.start()
    energies, n = own.shape[0], ham.shape[-1]
    rank = lax.axis_index("slab")
    sizes = [lax.axis_size(axis) for axis in ENERGY]
    place = [lax.axis_index(axis) for axis in ENERGY]
    devices = sizes[0] * sizes[1] * sizes[2]
    index = (place[0] * sizes[1] + place[1]) * sizes[2] + place[2]

    def along(step):
        other = lax.rem(index + step, devices)
        return (lax.div(other, sizes[1] * sizes[2]), lax.rem(lax.div(other, sizes[2]), sizes[1]), lax.rem(other, sizes[2]), rank)

    following, previous = along(1), along(devices - 1)
    partner = (*place, 1 - rank)
    lines = [
        [(*place[:a], lax.rem(place[a] + step, sizes[a]), *place[a + 1 :], rank) for step in range(1, sizes[a])]
        for a in range(3)
    ]
    barrier = pltpu.get_barrier_semaphore()
    peers = [following, previous, partner] + lines[0] + lines[1] + lines[2]
    for peer in peers:
        pl.semaphore_signal(barrier, inc=1, device_id=peer, device_id_type=MESH)

    pl.semaphore_wait(barrier, len(peers))

    def remote(source, target, send, recv, device):
        return pltpu.make_async_remote_copy(source, target, send, recv, device_id=device, device_id_type=MESH)

    halo = [
        remote(own_in, before, halo_send.at[0], halo_recv.at[0], following),
        remote(own_in, after, halo_send.at[1], halo_recv.at[1], previous),
    ]
    near = [
        remote(coupling_in.at[0], near_w, near_send.at[0], near_recv.at[0], partner),
        remote(bonds_in, near_b, near_send.at[1], near_recv.at[1], partner),
    ]
    for copy in halo + near:
        copy.start()
    diagonal = eye(n)
    for load in loads[:2]:
        load.wait()
    w_near = coupling[0] * bonds[0:1, :].astype(jnp.float32)
    v = coupling[1] * bonds[1:2, :].astype(jnp.float32)
    v = jnp.where(rank == 0, v, v.T)
    lead = jnp.where(rank == 0, product(w_near, w_near, ROWS), jnp.where(diagonal, LEAD_WIDTH, 0.0))
    for load in loads[2:]:
        load.wait()
    for copy in halo:
        copy.wait()

    points = [
        -HALF_WINDOW + 2.0 * HALF_WINDOW * ((index * energies + e).astype(jnp.float32) + 0.5) / (devices * energies)
        for e in range(energies)
    ]
    has_before, has_after = index > 0, index < devices - 1

    def build(slab):
        one = shifts[slab] == 1
        around = [jnp.where(has_before, before[e, slab], 0.0) for e in range(energies)]
        around += [own[e, slab] for e in range(energies)]
        around += [jnp.where(has_after, after[e, slab], 0.0) for e in range(energies)]
        blocks = []
        for e in range(energies):
            far, close, close_up, far_up = [around[energies + e + step] for step in (-2, -1, 1, 2)]
            self_energy = strength[pl.ds(slab, 1), :] * jnp.where(one, close + close_up, far + far_up)
            re = jnp.where(diagonal, points[e] - self_energy[0:1, :], 0.0) - ham[slab]
            im = jnp.where(diagonal, BROADENING - self_energy[1:2, :], 0.0)
            blocks.append((re, im))
        return blocks

    for e, (re, im) in enumerate(build(rank)):
        real[e] = re
        imag[e] = im + lead
    invert(real, imag)
    inner = build(1 - rank)
    for e in range(energies):
        xr, xi = -real[e], -imag[e]
        outer_x[e, 0] = xr
        outer_x[e, 1] = xi
        t = product(v, jnp.concatenate([xr, xi], axis=1), ROWS)
        outer_u[e, 0] = t[:, :n]
        outer_u[e, 1] = t[:, n:]
        self_energy = product(jnp.concatenate([t[:, :n], t[:, n:]], axis=0), v)
        re = inner[e][0] - self_energy[:n]
        im = inner[e][1] - self_energy[n:]
        inner_s[e, 0] = re
        inner_s[e, 1] = im
        real[e] = re
        imag[e] = im
    invert(real, imag)
    for e in range(energies):
        send_x[e, 0] = -real[e]
        send_x[e, 1] = -imag[e]
    swap = remote(send_x, recv_x, x_send.at[0], x_recv.at[0], partner)
    swap.start()
    for copy in near:
        copy.wait()
    theirs = near_w[...] * near_b[0:1, :].astype(jnp.float32)
    u = jnp.where(rank == 0, theirs.T, w_near)
    swap.wait()
    for e in range(energies):
        t = product(jnp.concatenate([recv_x[e, 0], recv_x[e, 1]], axis=0), u)
        self_energy = product(u, jnp.concatenate([t[:n], t[n:]], axis=1), ROWS)
        real[e] = inner_s[e, 0] - self_energy[:, :n]
        imag[e] = inner_s[e, 1] - self_energy[:, n:]
    invert(real, imag)
    sums = [jnp.zeros((1, n), jnp.float32), jnp.zeros((1, n), jnp.float32)]
    halves = []
    for e in range(energies):
        gr, gi = -real[e], -imag[e]
        ur, ui = outer_u[e, 0], outer_u[e, 1]
        y = product(jnp.concatenate([gr, gi], axis=0), jnp.concatenate([ur, ui], axis=1))
        yr, yi = y[:n, :n] - y[n:, n:], y[:n, n:] + y[n:, :n]
        halves.append((yr, yi))
        outer = outer_x[e, 1] * jnp.where(diagonal, 1.0, 0.0) + (ur * yi + ui * yr)
        occupied = 1.0 / (1.0 + jnp.exp(jnp.full((1, n), points[e] / THERMAL, jnp.float32)))
        sums[0] += occupied * jnp.sum(outer, axis=0, keepdims=True)
        sums[1] += occupied * jnp.sum(jnp.where(diagonal, gi, 0.0), axis=0, keepdims=True)
    partials[0, pl.ds(rank, 1), :] = sums[0]
    partials[0, pl.ds(1 - rank, 1), :] = sums[1]

    def finish():
        for e in range(energies):
            green[e, 1 - rank, 0] = -real[e]
            green[e, 1 - rank, 1] = -imag[e]
            yr, yi = halves[e]
            ur, ui = outer_u[e, 0], outer_u[e, 1]
            left = jnp.concatenate([jnp.concatenate([ur, ui], axis=1), jnp.concatenate([-ui, ur], axis=1)], axis=0)
            z = product(left, jnp.concatenate([yr, yi], axis=0), ROWS)
            green[e, rank, 0] = outer_x[e, 0] + z[:n]
            green[e, rank, 1] = outer_x[e, 1] + z[n:]

    sent = []
    buffers = [line_0, line_1, line_2]
    arrivals = [line_recv_0, line_recv_1, line_recv_2]
    for stage, a in enumerate((2, 1, 0)):
        buffer, arrival, mine = buffers[a], arrivals[a], place[a]
        source = partials.at[stage]
        copies = [
            remote(source, buffer.at[mine], line_send.at[a, step], arrival.at[mine], device)
            for step, device in enumerate(lines[a])
        ]
        for copy in copies:
            copy.start()
        sent += copies
        buffer[mine] = partials[stage]
        if stage == 0:
            finish()
        for step in range(1, sizes[a]):
            sender = lax.rem(mine + step, sizes[a])
            remote(source, buffer.at[sender], line_send.at[a, step - 1], arrival.at[sender], lines[a][step - 1]).wait_recv()
        total = buffer[0]
        for other in range(1, sizes[a]):
            total = total + buffer[other]
        if stage < 2:
            partials[stage + 1] = total
        else:
            density[...] = (-2.0 * HALF_WINDOW / (devices * energies) / jnp.pi) * total
    for copy in sent:
        copy.wait_send()


def write(green, density, green_out, density_out, sem):
    copies = [
        pltpu.make_async_copy(density, density_out, sem.at[0]),
        pltpu.make_async_copy(green, green_out, sem.at[1]),
    ]
    for copy in copies:
        copy.start()
    for copy in copies:
        copy.wait()


def shards(hamiltonian, coupling, bonds, phonon_coupling, previous_green, phonon_shift):
    energies, slabs, n = previous_green.shape[0], hamiltonian.shape[0], hamiltonian.shape[1]
    sizes = [lax.axis_size(axis) for axis in ENERGY]
    longest = max(sizes)
    block = pltpu.VMEM((energies, 2, n, n), jnp.float32)
    square = pltpu.VMEM((energies, n, n), jnp.float32)
    halo = pltpu.VMEM(previous_green.shape, jnp.float32)
    dma = pltpu.SemaphoreType.DMA
    results = (
        jax.ShapeDtypeStruct((energies, slabs, 2, n, n), jnp.float32),
        jax.ShapeDtypeStruct((slabs, n), jnp.float32),
    )
    found = pl.pallas_call(
        sweep,
        out_shape=results,
        in_specs=[HBM] * 6,
        out_specs=(VMEM, VMEM),
        scratch_shapes=[
            *[pltpu.VMEM(x.shape, x.dtype) for x in (hamiltonian, coupling, bonds, phonon_coupling)],
            pltpu.SMEM(phonon_shift.shape, jnp.int32), halo, halo, halo, pltpu.VMEM((n, n), jnp.float32), pltpu.VMEM(bonds.shape, jnp.int32),
            block, block, block, block, block, square, square,
            pltpu.VMEM((3, slabs, n), jnp.float32),
            *[pltpu.VMEM((size, slabs, n), jnp.float32) for size in sizes],
            dma((2,)), dma((2,)), dma((2,)), dma((2,)), dma((1,)), dma((1,)),
            dma((3, longest)), *[dma((size,)) for size in sizes], dma((6,)),
        ],
        compiler_params=pltpu.CompilerParams(collective_id=0, has_side_effects=True, vmem_limit_bytes=16 << 20),
        name="sweep",
    )(*[
        pltpu.with_memory_space_constraint(x, pltpu.HBM)
        for x in (hamiltonian, coupling, bonds, phonon_coupling, phonon_shift, previous_green)
    ])
    return pl.pallas_call(
        write,
        out_shape=results,
        in_specs=[VMEM] * 2,
        out_specs=(HBM, HBM),
        scratch_shapes=[dma((2,))],
        compiler_params=pltpu.CompilerParams(vmem_limit_bytes=16 << 20),
        name="write",
    )(*found)


def solution(mesh):
    split_mesh = Mesh(mesh.devices.reshape(8, 8, 4, mesh.shape["slab"]), (*ENERGY, "slab"))
    in_specs = (
        P("slab", None, None),
        P("slab", None, None),
        P("slab", None),
        P("slab", None),
        P(ENERGY, "slab", None, None),
        P("slab"),
    )
    out_specs = (P(ENERGY, "slab", None, None, None), P("slab", None))
    return jax.shard_map(shards, mesh=split_mesh, in_specs=in_specs, out_specs=out_specs, check_vma=False)
```

```python
import functools

import jax
import jax.numpy as jnp
from jax import lax
from jax.experimental import pallas as pl
from jax.experimental.pallas import tpu as pltpu
from jax.sharding import Mesh
from jax.sharding import PartitionSpec as P

ENERGY = ("energy_0", "energy_1", "energy_2")
MESH = pl.DeviceIdType.MESH
BROADENING = 0.2
LEAD_WIDTH = 0.5
THERMAL = 0.1
HALF_WINDOW = 3.0
GROUP = 8
ROWS = (((0,), (0,)), ((), ()))
PLAIN = (((1,), (0,)), ((), ()))
COLUMNS = (((1,), (1,)), ((), ()))
VMEM = pl.BlockSpec(memory_space=pltpu.VMEM)
HBM = pl.BlockSpec(memory_space=pltpu.HBM)


def split(x):
    high = x.astype(jnp.bfloat16)
    return high, (x - high.astype(jnp.float32)).astype(jnp.bfloat16)


def thirds(x):
    parts = []
    for _ in range(3):
        parts.append(x.astype(jnp.bfloat16))
        x = x - parts[-1].astype(jnp.float32)
    return parts


def dot(left, right, dims=PLAIN):
    return lax.dot_general(left, right, dims, preferred_element_type=jnp.float32)


def product(left, right, dims=PLAIN):
    (lh, ll), (rh, rl) = split(left), split(right)
    return dot(lh, rh, dims) + (dot(ll, rh, dims) + dot(lh, rl, dims))


def eye(n):
    return lax.broadcasted_iota(jnp.int32, (n, n), 0) == lax.broadcasted_iota(jnp.int32, (n, n), 1)


def times(a, b):
    return a[0] * b[0] - a[1] * b[1], a[0] * b[1] + a[1] * b[0]


def minus(a, b):
    return a[0] - b[0], a[1] - b[1]


def spread(x, k):
    return tuple(jnp.broadcast_to(part[k : k + 1, :], part.shape) for part in x)


def total_of(parts):
    while len(parts) > 1:
        parts = [parts[i] + parts[i + 1] for i in range(0, len(parts), 2)]
    return parts[0]


def invert(real, imag):
    energies, n = range(real.shape[0]), real.shape[-1]
    shape = (GROUP, n)
    lane = lax.broadcasted_iota(jnp.int32, shape, 1)
    row = lax.broadcasted_iota(jnp.int32, shape, 0)

    def column(x, j):
        return tuple(
            jnp.broadcast_to(jnp.sum(jnp.where(lane == j, part, 0.0), axis=1, keepdims=True), shape) for part in x
        )

    def load(e, at):
        return real[e, at : at + GROUP, :], imag[e, at : at + GROUP, :]

    current = [load(e, 0) for e in energies]
    for first in range(0, n, GROUP):
        inside = (lane >= first) & (lane < first + GROUP)
        unit = jnp.where(lane == first + row, 1.0, 0.0)
        before = current
        pivots = [[column(before[e], first + k) for k in range(GROUP)] for e in energies]
        solved = [(jnp.where(inside, unit, before[e][0]), jnp.where(inside, 0.0, before[e][1])) for e in energies]
        second = first + GROUP
        if second < n:
            following = [load(e, second) for e in energies]
            columns = [[column(following[e], first + k) for k in range(GROUP)] for e in energies]
        for k in range(GROUP):
            for e in energies:
                c = pivots[e][k]
                p = spread(c, k)
                d = 1.0 / (p[0] * p[0] + p[1] * p[1])
                q = (p[0] * d, -(p[1] * d))
                w = times(c, q)
                w = (jnp.where(row == k, 1.0 - q[0], w[0]), jnp.where(row == k, -q[1], w[1]))
                for j in range(k + 1, GROUP):
                    pivots[e][j] = minus(pivots[e][j], times(w, spread(pivots[e][j], k)))
                solved[e] = minus(solved[e], times(w, spread(solved[e], k)))
        current = []
        for e in energies:
            swept = tuple(jnp.where(inside, -part, part) for part in solved[e])
            if second < n:
                terms = [times(columns[e][k], spread(swept, k)) for k in range(GROUP)]
                rest = tuple(jnp.where(inside, 0.0, part) for part in following[e])
                current.append(minus(rest, (total_of([t[0] for t in terms]), total_of([t[1] for t in terms]))))
            left = thirds(jnp.concatenate(before[e], axis=0))
            right = [pair(x, y) for x, y in zip(thirds(swept[0] + unit), thirds(swept[1]))]
            which = ((0, 0), (1, 0), (2, 0), (0, 1), (1, 1), (0, 2))
            update = dot(
                jnp.concatenate([left[i] for i, _ in which], axis=0),
                jnp.concatenate([right[j] for _, j in which], axis=0),
                ROWS,
            )
            for at in [*range(second + GROUP, n, GROUP), *range(0, first, GROUP)]:
                s = slice(at, at + GROUP)
                real[e, s, :] = real[e, s, :] - update[s, :n]
                imag[e, s, :] = imag[e, s, :] - update[s, n:]
            real[e, first:second, :], imag[e, first:second, :] = swept


def pair(real, imag):
    return jnp.concatenate(
        [jnp.concatenate([real, imag], axis=1), jnp.concatenate([-imag, real], axis=1)], axis=0
    )


def sweep(
    ham_in, coupling_in, bonds_in, strength_in, shifts_in, own_in, green, density,
    ham, coupling, bonds, strength, shifts, own, before, after, near_w, near_b, outer_x, outer_u, inner_s, send_x, recv_x, real, imag,
    partials, plane_parts, line_parts, halo_send, halo_recv, near_send, near_recv, x_send, x_recv,
    part_send, plane_recv, line_recv, load_sem,
):
    loads = [
        pltpu.make_async_copy(source, target, load_sem.at[i])
        for i, (source, target) in enumerate(
            ((coupling_in, coupling), (bonds_in, bonds), (own_in, own), (strength_in, strength), (shifts_in, shifts), (ham_in, ham))
        )
    ]
    for load in loads:
        load.start()
    energies, n = own.shape[0], ham.shape[-1]
    rank = lax.axis_index("slab")
    sizes = [lax.axis_size(axis) for axis in ENERGY]
    place = [lax.axis_index(axis) for axis in ENERGY]
    devices = sizes[0] * sizes[1] * sizes[2]
    index = (place[0] * sizes[1] + place[1]) * sizes[2] + place[2]

    def along(step):
        other = lax.rem(index + step, devices)
        return (lax.div(other, sizes[1] * sizes[2]), lax.rem(lax.div(other, sizes[2]), sizes[1]), lax.rem(other, sizes[2]), rank)

    following, previous = along(1), along(devices - 1)
    partner = (*place, 1 - rank)
    plane = [
        (place[0], lax.rem(place[1] + y, sizes[1]), lax.rem(place[2] + x, sizes[2]), rank)
        for y in range(sizes[1])
        for x in range(sizes[2])
        if y or x
    ]
    line = [(lax.rem(place[0] + step, sizes[0]), place[1], place[2], rank) for step in range(1, sizes[0])]
    barrier = pltpu.get_barrier_semaphore()
    peers = [following, previous, partner] + plane + line
    for peer in peers:
        pl.semaphore_signal(barrier, inc=1, device_id=peer, device_id_type=MESH)

    pl.semaphore_wait(barrier, len(peers))

    def remote(source, target, send, recv, device):
        return pltpu.make_async_remote_copy(source, target, send, recv, device_id=device, device_id_type=MESH)

    halo = [
        remote(own_in, before, halo_send.at[0], halo_recv.at[0], following),
        remote(own_in, after, halo_send.at[1], halo_recv.at[1], previous),
    ]
    near = [
        remote(coupling_in.at[0], near_w, near_send.at[0], near_recv.at[0], partner),
        remote(bonds_in, near_b, near_send.at[1], near_recv.at[1], partner),
    ]
    for copy in halo + near:
        copy.start()
    diagonal = eye(n)
    for load in loads[:2]:
        load.wait()
    w_near = coupling[0] * bonds[0:1, :].astype(jnp.float32)
    v = coupling[1] * bonds[1:2, :].astype(jnp.float32)
    v = jnp.where(rank == 0, v, v.T)
    lead = jnp.where(rank == 0, product(w_near, w_near, ROWS), jnp.where(diagonal, LEAD_WIDTH, 0.0))
    for load in loads[2:]:
        load.wait()
    for copy in halo:
        copy.wait()

    points = [
        -HALF_WINDOW + 2.0 * HALF_WINDOW * ((index * energies + e).astype(jnp.float32) + 0.5) / (devices * energies)
        for e in range(energies)
    ]
    has_before, has_after = index > 0, index < devices - 1

    def build(slab):
        one = shifts[slab] == 1
        around = [jnp.where(has_before, before[e, slab], 0.0) for e in range(energies)]
        around += [own[e, slab] for e in range(energies)]
        around += [jnp.where(has_after, after[e, slab], 0.0) for e in range(energies)]
        blocks = []
        for e in range(energies):
            far, close, close_up, far_up = [around[energies + e + step] for step in (-2, -1, 1, 2)]
            self_energy = strength[pl.ds(slab, 1), :] * jnp.where(one, close + close_up, far + far_up)
            re = jnp.where(diagonal, points[e] - self_energy[0:1, :], 0.0) - ham[slab]
            im = jnp.where(diagonal, BROADENING - self_energy[1:2, :], 0.0)
            blocks.append((re, im))
        return blocks

    for e, (re, im) in enumerate(build(rank)):
        real[e] = re
        imag[e] = im + lead
    invert(real, imag)
    inner = build(1 - rank)
    for e in range(energies):
        xr, xi = -real[e], -imag[e]
        outer_x[e, 0] = xr
        outer_x[e, 1] = xi
        t = product(v, jnp.concatenate([xr, xi], axis=1), ROWS)
        outer_u[e, 0] = t[:, :n]
        outer_u[e, 1] = t[:, n:]
        self_energy = product(jnp.concatenate([t[:, :n], t[:, n:]], axis=0), v)
        re = inner[e][0] - self_energy[:n]
        im = inner[e][1] - self_energy[n:]
        inner_s[e, 0] = re
        inner_s[e, 1] = im
        real[e] = re
        imag[e] = im
    invert(real, imag)
    for e in range(energies):
        send_x[e, 0] = -real[e]
        send_x[e, 1] = -imag[e]
    swap = remote(send_x, recv_x, x_send.at[0], x_recv.at[0], partner)
    swap.start()
    for copy in near:
        copy.wait()
    theirs = near_w[...] * near_b[0:1, :].astype(jnp.float32)
    u = jnp.where(rank == 0, theirs.T, w_near)
    swap.wait()
    for e in range(energies):
        t = product(jnp.concatenate([recv_x[e, 0], recv_x[e, 1]], axis=0), u)
        self_energy = product(u, jnp.concatenate([t[:n], t[n:]], axis=1), ROWS)
        real[e] = inner_s[e, 0] - self_energy[:, :n]
        imag[e] = inner_s[e, 1] - self_energy[:, n:]
    invert(real, imag)
    sums = [jnp.zeros((1, n), jnp.float32), jnp.zeros((1, n), jnp.float32)]
    halves = []
    for e in range(energies):
        gr, gi = -real[e], -imag[e]
        ur, ui = outer_u[e, 0], outer_u[e, 1]
        y = product(jnp.concatenate([gr, gi], axis=0), jnp.concatenate([ur, ui], axis=1))
        yr, yi = y[:n, :n] - y[n:, n:], y[:n, n:] + y[n:, :n]
        halves.append((yr, yi))
        outer = outer_x[e, 1] * jnp.where(diagonal, 1.0, 0.0) + (ur * yi + ui * yr)
        occupied = 1.0 / (1.0 + jnp.exp(jnp.full((1, n), points[e] / THERMAL, jnp.float32)))
        sums[0] += occupied * jnp.sum(outer, axis=0, keepdims=True)
        sums[1] += occupied * jnp.sum(jnp.where(diagonal, gi, 0.0), axis=0, keepdims=True)
    partials[0, pl.ds(rank, 1), :] = sums[0]
    partials[0, pl.ds(1 - rank, 1), :] = sums[1]

    def finish():
        for e in range(energies):
            green[e, 1 - rank, 0] = -real[e]
            green[e, 1 - rank, 1] = -imag[e]
            yr, yi = halves[e]
            ur, ui = outer_u[e, 0], outer_u[e, 1]
            left = jnp.concatenate([jnp.concatenate([ur, ui], axis=1), jnp.concatenate([-ui, ur], axis=1)], axis=0)
            z = product(left, jnp.concatenate([yr, yi], axis=0), ROWS)
            green[e, rank, 0] = outer_x[e, 0] + z[:n]
            green[e, rank, 1] = outer_x[e, 1] + z[n:]

    sent = []

    def in_plane(device):
        return device[1] * sizes[2] + device[2]

    def in_line(device):
        return device[0]

    for stage, (group, slot, parts, arrival) in enumerate(
        ((plane, in_plane, plane_parts, plane_recv), (line, in_line, line_parts, line_recv))
    ):
        source, mine = partials.at[stage], slot((*place, rank))
        copies = [
            remote(source, parts.at[mine], part_send.at[stage, i], arrival.at[mine], device)
            for i, device in enumerate(group)
        ]
        for copy in copies:
            copy.start()
        sent += copies
        parts[mine] = partials[stage]
        if stage == 0:
            finish()
        for i, device in enumerate(group):
            sender = slot(device)
            remote(source, parts.at[sender], part_send.at[stage, i], arrival.at[sender], device).wait_recv()
        total = total_of([parts[i] for i in range(len(group) + 1)])
        if stage == 0:
            partials[1] = total
        else:
            density[...] = (-2.0 * HALF_WINDOW / (devices * energies) / jnp.pi) * total
    for copy in sent:
        copy.wait_send()


def write(green, density, green_out, density_out, sem):
    copies = [
        pltpu.make_async_copy(density, density_out, sem.at[0]),
        pltpu.make_async_copy(green, green_out, sem.at[1]),
    ]
    for copy in copies:
        copy.start()
    for copy in copies:
        copy.wait()


def shards(hamiltonian, coupling, bonds, phonon_coupling, previous_green, phonon_shift):
    energies, slabs, n = previous_green.shape[0], hamiltonian.shape[0], hamiltonian.shape[1]
    sizes = [lax.axis_size(axis) for axis in ENERGY]
    places = (sizes[1] * sizes[2], sizes[0])
    block = pltpu.VMEM((energies, 2, n, n), jnp.float32)
    square = pltpu.VMEM((energies, n, n), jnp.float32)
    halo = pltpu.VMEM(previous_green.shape, jnp.float32)
    dma = pltpu.SemaphoreType.DMA
    results = (
        jax.ShapeDtypeStruct((energies, slabs, 2, n, n), jnp.float32),
        jax.ShapeDtypeStruct((slabs, n), jnp.float32),
    )
    found = pl.pallas_call(
        sweep,
        out_shape=results,
        in_specs=[HBM] * 6,
        out_specs=(VMEM, VMEM),
        scratch_shapes=[
            *[pltpu.VMEM(x.shape, x.dtype) for x in (hamiltonian, coupling, bonds, phonon_coupling)],
            pltpu.SMEM(phonon_shift.shape, jnp.int32), halo, halo, halo, pltpu.VMEM((n, n), jnp.float32), pltpu.VMEM(bonds.shape, jnp.int32),
            block, block, block, block, block, square, square,
            pltpu.VMEM((2, slabs, n), jnp.float32),
            *[pltpu.VMEM((size, slabs, n), jnp.float32) for size in places],
            dma((2,)), dma((2,)), dma((2,)), dma((2,)), dma((1,)), dma((1,)),
            dma((2, max(places))), *[dma((size,)) for size in places], dma((6,)),
        ],
        compiler_params=pltpu.CompilerParams(collective_id=0, has_side_effects=True, vmem_limit_bytes=16 << 20),
        name="sweep",
    )(*[
        pltpu.with_memory_space_constraint(x, pltpu.HBM)
        for x in (hamiltonian, coupling, bonds, phonon_coupling, phonon_shift, previous_green)
    ])
    return pl.pallas_call(
        write,
        out_shape=results,
        in_specs=[VMEM] * 2,
        out_specs=(HBM, HBM),
        scratch_shapes=[dma((2,))],
        compiler_params=pltpu.CompilerParams(vmem_limit_bytes=16 << 20),
        name="write",
    )(*found)


def solution(mesh):
    split_mesh = Mesh(mesh.devices.reshape(8, 8, 4, mesh.shape["slab"]), (*ENERGY, "slab"))
    in_specs = (
        P("slab", None, None),
        P("slab", None, None),
        P("slab", None),
        P("slab", None),
        P(ENERGY, "slab", None, None),
        P("slab"),
    )
    out_specs = (P(ENERGY, "slab", None, None, None), P("slab", None))
    return jax.shard_map(shards, mesh=split_mesh, in_specs=in_specs, out_specs=out_specs, check_vma=False)
```
